256 devices in a mesh: gx: 32 (over z_hi, y, core), gy: 8 (over z_lo, x).
Axes of the slice: x: 4, y: 4, z: 8 (z_hi: 4, z_lo: 2; z = z_hi * 2 + z_lo), core: 2. Of those that a mesh axis runs over, the one named last changes fastest.
Arguments:
- species: float32 [48, 256, 128, 128], P(None, 'gx', 'gy'), may hold values from 0.2 to 2
- rate_matrices: float32 [256, 128, 2304], P('gx', 'gy'), may hold values from -20 to 10, as said below
- loss_rates: float32 [48], replicated, may hold values from 0.05 to 0.5
- sweeps: int32 [256, 128], P('gx', 'gy'), may hold values from 5 to 10, as said below
- flow_rows: float32 [256, 128, 128], P('gx', 'gy'), may hold values from -0.24 to 0.24
- flow_columns: float32 [256, 128, 128], P('gx', 'gy'), may hold values from -0.24 to 0.24
Outputs:
- transported: float32 [48, 256, 128, 128], P(None, 'gx', 'gy')
The draws below stay inside these ranges and needn't reach their ends.
Inputs may be any that keep to these rules, and one draw needn't show every extreme that they name: `rate_matrices`: each column's rate matrix times the time step, with a negative diagonal. Columns in rows 112 to 143 take 9 or 10 sweeps, all others 5 or 6; both 5 and 10 occur.
All inputs are finite; a program needn't handle non-finite values.
Results may differ from the reference program's by a relative error of at most 0.0003.
Values sent between devices are 32-bit elements; how exact they have to be, the bound alone decides.
No kernel may reach another device: no remote copies, remote signals or barrier semaphores. Data moves between devices by JAX's collectives and lax.ppermute only.
A program may use at most 128 MiB of HBM per device.

```python
import math
import jax
import jax.numpy as jnp
from jax import lax

S = 48
NZ = 128
MAX_SWEEPS = 10
NX = 256
NY = 128


def draw_rate_matrices(key, part):
    first_key, second_key = jax.random.split(key)
    decay = jnp.exp(jax.random.uniform(first_key, (NX, NY, S), jnp.float32, jnp.log(2.0), jnp.log(20.0)))
    coupled = jnp.clip(jax.random.normal(second_key, (NX, NY, S, S), jnp.float32), -4.0, 4.0)
    radius = 0.8
    gamma_value = 1.0 + 0.5 ** 0.5
    spread = radius / S ** 0.5 * (1.0 / gamma_value + decay)[..., None]
    identity = jnp.eye(S, dtype=jnp.float32)
    matrices = identity * -decay[..., None] + (1.0 - identity) * spread * coupled
    return matrices.reshape(NX, NY, S * S)


def draw_sweeps(key, part):
    first_key, second_key = jax.random.split(key)
    light = jax.random.randint(first_key, (NX, NY), 5, 7, dtype=jnp.int32)
    heavy = jax.random.randint(second_key, (NX, NY), 9, 11, dtype=jnp.int32)
    row_index = jnp.arange(NX, dtype=jnp.int32)[:, None]
    inside = (row_index >= NX // 2 - NX // 16) & (row_index < NX // 2 + NX // 16)
    counts = jnp.where(inside, heavy, light)
    counts = counts.at[NX // 2, 0].set(10)
    return counts.at[0, 0].set(5)


def steps_of(stream_key, extent, cuts, smallest, high):
    def one(position, parts):
        draws = jax.random.uniform(jax.random.fold_in(jax.random.fold_in(stream_key, 6), position), (parts,), jnp.float32, smallest / len(cuts), high / len(cuts))
        return jnp.repeat(jnp.exp(draws), extent[position] // parts).reshape((-1,) + (1,) * (len(extent) - position - 1))

    loudness = one(*cuts[0])
    for cut in cuts[1:]:
        loudness = loudness * one(*cut)
    return loudness


def setup_inputs(seed: int = 0) -> dict:
    seeds = jax.random.split(jax.random.key(seed), 7)
    return {
        "species": jnp.clip(jnp.exp(math.log(2.0) - 2.3025851 * jax.random.uniform(seeds[0], (S, NX, NY, NZ), jnp.float32) ** steps_of(seeds[0], (S, NX, NY, NZ), ((1, 32), (2, 8)), -0.2, 0.2)), 0.2, 2.0),
        "rate_matrices": draw_rate_matrices(jax.random.fold_in(seeds[6], 71), 0),
        "loss_rates": jnp.clip(jnp.exp(jax.random.uniform(seeds[2], (S,), jnp.float32, math.log(0.05), math.log(0.5))), 0.05, 0.5),
        "sweeps": draw_sweeps(jax.random.fold_in(seeds[6], 71), 0),
        "flow_rows": jnp.clip(jax.random.uniform(seeds[4], (NX, NY, NZ), jnp.float32, -0.24, 0.24) * steps_of(seeds[4], (NX, NY, NZ), ((0, 32), (1, 8)), -0.4, 0.0), -0.24, 0.24),
        "flow_columns": jnp.clip(jax.random.uniform(seeds[5], (NX, NY, NZ), jnp.float32, -0.24, 0.24) * steps_of(seeds[5], (NX, NY, NZ), ((0, 32), (1, 8)), -0.4, 0.0), -0.24, 0.24),
    }


section_gamma = 1.0 + 0.5 ** 0.5


def linear_parts(matrices):
    species_count = matrices.shape[-1]
    identity = jnp.eye(species_count, dtype=jnp.float32)
    diagonal = jnp.sum(matrices * identity, axis=-1)
    coupling = section_gamma * (matrices * (1.0 - identity))
    scaled = 1.0 - section_gamma * diagonal
    return coupling, scaled


def product(matrices, values):
    return jnp.einsum('bij,bjn->bin', matrices, values, precision=lax.Precision.HIGHEST)


def tendency(matrices, values, loss_rates):
    return product(matrices, values) - loss_rates[:, None] * values * values


def advect(concentration, flow_first, flow_second):
    row_flux = jnp.maximum(flow_first[:-1], 0.0) * concentration[:, :-1] + jnp.minimum(flow_first[:-1], 0.0) * concentration[:, 1:]
    column_flux = jnp.maximum(flow_second[:, :-1], 0.0) * concentration[:, :, :-1] + jnp.minimum(flow_second[:, :-1], 0.0) * concentration[:, :, 1:]
    interior = concentration[:, 1:-1, 1:-1]
    return interior - (row_flux[:, 1:, 1:-1] - row_flux[:, :-1, 1:-1]) - (column_flux[:, 1:-1, 1:] - column_flux[:, 1:-1, :-1])


def reference(species, rate_matrices, loss_rates, sweeps, flow_rows, flow_columns):
    columns_first = jnp.transpose(species, (1, 2, 0, 3))
    matrices_all = rate_matrices.reshape(NX, NY, S, S)

    def react_row(pieces):
        values, matrices, counts = pieces
        coupling, scaled = linear_parts(matrices)

        def run_sweeps(source):
            solved = jnp.zeros_like(source)
            for sweep_index in range(MAX_SWEEPS):
                update = (source + product(coupling, solved)) / scaled[:, :, None]
                solved = jnp.where((sweep_index < counts)[:, None, None], update, solved)
            return solved

        section_one = run_sweeps(tendency(matrices, values, loss_rates))
        shifted = values + section_one
        second = run_sweeps(tendency(matrices, shifted, loss_rates) - 2.0 * section_one)
        return values + 1.5 * section_one + 0.5 * second

    reacted = lax.map(react_row, (columns_first, matrices_all, sweeps))
    reacted = jnp.transpose(reacted, (2, 0, 1, 3))
    flow_first = jnp.pad(flow_rows, ((1, 1), (1, 1), (0, 0)))
    flow_second = jnp.pad(flow_columns, ((1, 1), (1, 1), (0, 0)))

    def transport_one(single):
        current = single[None]
        for substep in range(2):
            padded = jnp.pad(current, ((0, 0), (1, 1), (1, 1), (0, 0)))
            current = advect(padded, flow_first, flow_second)
        return current[0]

    return lax.map(transport_one, reacted)
```

```python
import jax
import jax.numpy as jnp
from jax import lax
from jax.experimental import pallas as pl
from jax.experimental.pallas import tpu as pltpu
from jax.sharding import PartitionSpec as P

gamma = 1.0 + 0.5**0.5
species_count = 48
depth = 128
rows_here = 8
columns_here = 16
single = jnp.float32
half = jnp.bfloat16
vmem = 48 << 20


def left(matrix):
    high = matrix.astype(half).astype(single)
    first = (high + pltpu.roll(matrix - high, 64, 1)).astype(half)
    return jnp.concatenate([first, high.astype(half)[:, :species_count]], axis=1)


def right(values):
    high = values.astype(half)
    low = (values - high.astype(single)).astype(half)
    gap = jnp.zeros((16, values.shape[1]), half)
    return jnp.concatenate([high, gap, high, gap, low], axis=0)


def times(one, other):
    return jnp.dot(one, other, preferred_element_type=single)


def react_columns(loads, coefficients, loss, counts):
    every = range(len(loads))
    row = lax.broadcasted_iota(jnp.int32, (species_count, depth), 0)
    lane = lax.broadcasted_iota(jnp.int32, (species_count, depth), 1)
    eye = (row == lane).astype(single)
    inverse, one, left_one = [], [], []
    for c in every:
        matrix = coefficients[c]()
        scaled = 1.0 - gamma * jnp.sum(matrix * eye, axis=1, keepdims=True)
        inverse.append(1.0 / scaled)
        one.append((gamma * (matrix - matrix * eye)) * inverse[c])
        left_one.append(left(one[c]))
    two = [times(left_one[c], right(one[c])) for c in every]
    base = [times(left_one[c], right(loads[c]())) for c in every]
    left_two = [left(two[c]) for c in every]
    pair = [times(left_two[c], right(one[c] + pltpu.roll(two[c], 64, 1))) for c in every]
    three = [jnp.where(lane < species_count, pair[c], 0.0) for c in every]
    four = [jnp.where(lane < species_count, pltpu.roll(pair[c], 64, 1), 0.0) for c in every]
    five = [times(left_two[c], right(three[c])) for c in every]
    left_five = [left(five[c]) for c in every]
    rest = []
    for c in every:
        more = [(counts[c] > q).astype(single) for q in (5, 6, 7, 8, 9)]
        rest.append(
            eye * more[0] + one[c] * more[1] + two[c] * more[2] + three[c] * more[3] + four[c] * more[4]
        )
    high_part = [times(left_five[c], right(rest[c])) for c in every]
    left_sum = [left(eye + one[c] + two[c] + three[c] + four[c] + high_part[c]) for c in every]
    base = [(base[c] + (inverse[c] - 1.0) * loads[c]()) * (1.0 / gamma) for c in every]
    first = []
    for c in every:
        values = loads[c]()
        first.append(base[c] - (inverse[c] * loss) * (values * values))
    first = [times(left_sum[c], right(first[c])) for c in every]
    moved = [times(left_one[c], right(first[c])) for c in every]
    second = []
    for c in every:
        shifted = loads[c]() + first[c]
        second.append(
            base[c]
            + (moved[c] + (inverse[c] - 1.0) * first[c]) * (1.0 / gamma)
            - (inverse[c] * loss) * (shifted * shifted)
            - (2.0 * inverse[c]) * first[c]
        )
    second = [times(left_sum[c], right(second[c])) for c in every]
    return [loads[c]() + 1.5 * first[c] + 0.5 * second[c] for c in every]


def react_kernel(start, at_once, corner_row, counts_ref, x_ref, a_ref, loss_ref, fr_ref, fc_ref, o_ref, *rest):
    corner_ref, mats = rest if corner_row is not None else (None, rest[0])
    mats[...] = jnp.zeros_like(mats)
    for r in range(2):
        for h in range(2):
            for i in range(species_count):
                mats[r * 2 + h, 8 * i : 8 * i + 8, 0:species_count] = a_ref[
                    r, 8 * h : 8 * h + 8, species_count * i : species_count * i + species_count
                ]
    row = lax.broadcasted_iota(jnp.int32, (species_count, species_count), 0)
    lane = lax.broadcasted_iota(jnp.int32, (species_count, species_count), 1)
    loss = jnp.sum(jnp.where(row == lane, loss_ref[...], 0.0), axis=1, keepdims=True)
    flat = x_ref.reshape(species_count * 32, depth)
    for base in range(0, 32, at_once):
        span = range(base, base + at_once)
        results = react_columns(
            [(lambda c=c: flat[pl.ds(c, species_count, 32), :]) for c in span],
            [(lambda c=c: mats[c // 8, pl.ds(c % 8, species_count, 8), :]) for c in span],
            loss,
            [counts_ref[start + c // 16, c % 16] for c in span],
        )
        for c, result in zip(span, results):
            o_ref[c] = result
            if corner_row is not None and c // 16 == corner_row and c % 16 in (0, 15):
                corner_ref[(c % 16) // 15] = result
    if corner_row is not None:
        for k, ref in enumerate((fr_ref, fc_ref)):
            for r in range(2):
                o_ref[32 + k, 16 * r : 16 * r + 16, :] = ref[r]
            for e, column in enumerate((0, 15)):
                corner_ref[2, 8 * k + e : 8 * k + e + 1, :] = ref[corner_row, column : column + 1, :]


def react_rows(block, corner_row, species, matrices, loss, sweeps, flow_rows, flow_columns):
    total = 32 if corner_row is None else 34
    shapes = [jax.ShapeDtypeStruct((total, species_count, depth), single)]
    if corner_row is not None:
        shapes.append(jax.ShapeDtypeStruct((3, species_count, depth), single))
    spec = pltpu.PrefetchScalarGridSpec(
        num_scalar_prefetch=1,
        grid=(1,),
        in_specs=[
            pl.BlockSpec((species_count, 2, 16, depth), lambda g, _: (0, block, 0, 0)),
            pl.BlockSpec((2, 16, species_count**2), lambda g, _: (block, 0, 0)),
            pl.BlockSpec((1, species_count), lambda g, _: (0, 0)),
            pl.BlockSpec((2, 16, depth), lambda g, _: (block, 0, 0)),
            pl.BlockSpec((2, 16, depth), lambda g, _: (block, 0, 0)),
        ],
        out_specs=[pl.BlockSpec(s.shape, lambda g, _: (0, 0, 0)) for s in shapes],
        scratch_shapes=[pltpu.VMEM((4, 8 * species_count, depth), single)],
    )

    def body(*refs):
        react_kernel(2 * block, 16, corner_row, *refs)

    return pl.pallas_call(
        body,
        out_shape=shapes,
        grid_spec=spec,
        compiler_params=pltpu.CompilerParams(vmem_limit_bytes=vmem),
        name=f"react_{block}",
    )(sweeps, species, matrices, loss, flow_rows, flow_columns)


def pack_kernel(low, mid_a, mid_b, high, corner_up, corner_down, fr, fc, to_left, to_right, sems):
    copies = []

    def copy(source, target):
        k = len(copies)
        copies.append(pltpu.make_async_copy(source, target, sems.at[k]))
        copies[-1].start()

    for side, (target, column, corner) in enumerate(((to_left, 0, 0), (to_right, 14, 1))):
        for k, part in enumerate((low, mid_a, mid_b, high)):
            for r in range(2):
                first = 2 + (2 * k + r) * 2
                copy(part.at[pl.ds(16 * r + column, 2)], target.at[pl.ds(first, 2)])
        for first, part in ((0, corner_up), (18, corner_down)):
            copy(part.at[pl.ds(corner, 1)], target.at[pl.ds(first + corner, 1)])
    for side, (target, column, corner) in enumerate(((to_left, 0, 0), (to_right, 14, 1))):
        for k, flow in enumerate((fr, fc)):
            for r in range(8):
                first = 2 + 2 * r
                target[20 + k, first : first + 2, :] = flow[r, column : column + 2, :]
    for one in copies:
        one.wait()
    for side, (target, column, corner) in enumerate(((to_left, 0, 0), (to_right, 14, 1))):
        for k in range(2):
            for first, part in ((0, corner_up), (18, corner_down)):
                target[20 + k, first + corner : first + corner + 1, :] = part[
                    2, 8 * k + corner : 8 * k + corner + 1, :
                ]


def pack(low, mid_a, mid_b, high, corner_up, corner_down, flow_rows, flow_columns):
    inside = pl.BlockSpec(memory_space=pltpu.VMEM)
    outside = pl.BlockSpec(memory_space=pl.ANY)
    shape = jax.ShapeDtypeStruct((22, species_count, depth), single)
    return pl.pallas_call(
        pack_kernel,
        out_shape=[shape, shape],
        in_specs=[outside] * 4 + [inside] * 4,
        out_specs=[inside, inside],
        scratch_shapes=[pltpu.SemaphoreType.DMA((20,))],
        compiler_params=pltpu.CompilerParams(vmem_limit_bytes=vmem),
        name="pack",
    )(low, mid_a, mid_b, high, corner_up, corner_down, flow_rows, flow_columns)


def transport_kernel(
    inside_ref, low, mid_a, mid_b, high, above, below, before, after, fr_ref, fc_ref,
    o_ref, c, later, wide_rows, wide_columns, weights, extra, sems,
):
    g = pl.program_id(0)

    def step(source, target, r, columns, place):
        for j in columns:
            a = [weights[q, place, j : j + 1, :] for q in range(5)]
            yield j, (
                a[0] * source(0, j)
                + a[1] * source(-1, j)
                + a[2] * source(1, j)
                + a[3] * source(0, j - 1)
                + a[4] * source(0, j + 1)
            )

    def one_later(r):
        for j, value in step(lambda di, j: c[r + 1 + di, j + 1], later, r, range(18), r):
            later[r, j] = value

    @pl.when(g == 0)
    def _():
        copies = []

        def copy(source, target):
            k = len(copies)
            copies.append(pltpu.make_async_copy(source, target, sems.at[k]))
            copies[-1].start()

        for k, part in enumerate((above, low, mid_a, mid_b, high, below)):
            for r in range(2):
                copy(part.at[pl.ds(16 * r, 16)], c.at[2 * k + r, pl.ds(2, 16)])
        for part, column in ((before, 0), (after, 18)):
            for r in range(10):
                copy(part.at[pl.ds(2 * r, 2)], c.at[1 + r, pl.ds(column, 2)])
        for k, (part, start) in enumerate(((above, 32), (below, 32), (before, 20), (after, 20))):
            copy(part.at[pl.ds(start, 2)], extra.at[k])
        for one in copies:
            one.wait()
        for k, (wide, own) in enumerate(((wide_rows, fr_ref), (wide_columns, fc_ref))):
            wide[...] = jnp.zeros_like(wide)
            for r in range(8):
                wide[2 + r, 2:18, :] = own[r]
            for r in range(2):
                wide[r, 2:18, :] = extra[0, k, 16 * r : 16 * r + 16, :]
                wide[10 + r, 2:18, :] = extra[1, k, 16 * r : 16 * r + 16, :]
            for r in range(10):
                wide[1 + r, 0:2, :] = extra[2, k, 2 * r : 2 * r + 2, :]
                wide[1 + r, 18:20, :] = extra[3, k, 2 * r : 2 * r + 2, :]
        has = [inside_ref[q].astype(single) for q in range(4)]
        column = lax.broadcasted_iota(jnp.int32, (18, depth), 0)
        for r in range(10):
            rows_out, rows_in = wide_rows[r + 1, 1:19, :], wide_rows[r, 1:19, :]
            columns_out, columns_in = wide_columns[r + 1, 1:19, :], wide_columns[r + 1, 0:18, :]
            kept = jnp.where(column == 0, has[2], jnp.where(column == 17, has[3], 1.0))
            if r == 0:
                kept = kept * has[0]
            if r == 9:
                kept = kept * has[1]
            outward = (
                jnp.maximum(rows_out, 0.0)
                - jnp.minimum(rows_in, 0.0)
                + jnp.maximum(columns_out, 0.0)
                - jnp.minimum(columns_in, 0.0)
            )
            for q, weight in enumerate(
                (
                    1.0 - outward,
                    jnp.maximum(rows_in, 0.0),
                    -jnp.minimum(rows_out, 0.0),
                    jnp.maximum(columns_in, 0.0),
                    -jnp.minimum(columns_out, 0.0),
                )
            ):
                weights[q, r, 0:18, :] = kept * weight
        for r in range(10):
            one_later(r)


    flat = o_ref.reshape(species_count * 16, depth)
    for j, value in step(lambda di, j: later[g + 1 + di, j], o_ref, g, range(1, 17), g + 1):
        flat[pl.ds(j - 1, species_count, 16), :] = value


def transport(inside, low, mid_a, mid_b, high, above, below, before, after, flow_rows, flow_columns):
    outside = pl.BlockSpec(memory_space=pl.ANY)
    flow = pl.BlockSpec((8, 16, depth), lambda g, _: (0, 0, 0))
    spec = pltpu.PrefetchScalarGridSpec(
        num_scalar_prefetch=1,
        grid=(8,),
        in_specs=[outside] * 8 + [flow, flow],
        out_specs=pl.BlockSpec((species_count, 1, 16, depth), lambda g, _: (0, g, 0, 0)),
        scratch_shapes=[
            pltpu.VMEM((12, 20, species_count, depth), single),
            pltpu.VMEM((10, 18, species_count, depth), single),
            pltpu.VMEM((12, 24, depth), single),
            pltpu.VMEM((12, 24, depth), single),
            pltpu.VMEM((5, 10, 24, depth), single),
            pltpu.VMEM((4, 2, species_count, depth), single),
            pltpu.SemaphoreType.DMA((36,)),
        ],
    )
    return pl.pallas_call(
        transport_kernel,
        out_shape=jax.ShapeDtypeStruct((species_count, rows_here, columns_here, depth), single),
        grid_spec=spec,
        compiler_params=pltpu.CompilerParams(vmem_limit_bytes=vmem),
        name="transport",
    )(inside, low, mid_a, mid_b, high, above, below, before, after, flow_rows, flow_columns)


def onward(array, axis, by):
    length = lax.axis_size(axis)
    pairs = [(i, i + by) for i in range(length) if 0 <= i + by < length]
    return lax.ppermute(array, axis, pairs)


def on_device(species, rate_matrices, loss_rates, sweeps, flow_rows, flow_columns):
    loss = loss_rates.reshape(1, species_count)
    arguments = (species, rate_matrices, loss, sweeps, flow_rows, flow_columns)
    high, high_corner = react_rows(3, 1, *arguments)
    low, low_corner = react_rows(0, 0, *arguments)
    corner_up = onward(high_corner, "gx", 1)
    corner_down = onward(low_corner, "gx", -1)
    above = onward(high, "gx", 1)
    below = onward(low, "gx", -1)
    (mid_a,) = react_rows(1, None, *arguments)
    (mid_b,) = react_rows(2, None, *arguments)
    to_left, to_right = pack(low, mid_a, mid_b, high, corner_up, corner_down, flow_rows, flow_columns)
    before = onward(to_right, "gy", 1)
    after = onward(to_left, "gy", -1)
    x, y = lax.axis_index("gx"), lax.axis_index("gy")
    inside = jnp.stack(
        [x > 0, x < lax.axis_size("gx") - 1, y > 0, y < lax.axis_size("gy") - 1]
    ).astype(jnp.int32)
    return transport(inside, low, mid_a, mid_b, high, above, below, before, after, flow_rows, flow_columns)


def solution(mesh):
    placed = (
        P(None, "gx", "gy", None),
        P("gx", "gy", None),
        P(),
        P("gx", "gy"),
        P("gx", "gy", None),
        P("gx", "gy", None),
    )
    return jax.shard_map(
        on_device, mesh=mesh, in_specs=placed, out_specs=P(None, "gx", "gy", None), check_vma=False
    )
```

```python
import jax
import jax.numpy as jnp
from jax import lax
from jax.experimental import pallas as pl
from jax.experimental.pallas import tpu as pltpu
from jax.sharding import PartitionSpec as P

gamma = 1.0 + 0.5**0.5
species_count = 48
depth = 128
rows_here = 8
columns_here = 16
single = jnp.float32
half = jnp.bfloat16
vmem = 40 << 20
vmem_small = 16 << 20


def left(matrix):
    high = matrix.astype(half).astype(single)
    first = (high + pltpu.roll(matrix - high, 64, 1)).astype(half)
    return jnp.concatenate([first, high.astype(half)[:, :species_count]], axis=1)


def right(values):
    high = values.astype(half)
    low = (values - high.astype(single)).astype(half)
    gap = jnp.zeros((16, values.shape[1]), half)
    return jnp.concatenate([high, gap, high, gap, low], axis=0)


def times(one, other):
    return jnp.dot(one, other, preferred_element_type=single)


def react_columns(loads, coefficients, loss, counts):
    every = range(len(loads))
    row = lax.broadcasted_iota(jnp.int32, (species_count, depth), 0)
    lane = lax.broadcasted_iota(jnp.int32, (species_count, depth), 1)
    eye = (row == lane).astype(single)
    inverse, one, left_one = [], [], []
    for c in every:
        matrix = coefficients[c]()
        scaled = 1.0 - gamma * jnp.sum(matrix * eye, axis=1, keepdims=True)
        inverse.append(1.0 / scaled)
        one.append((gamma * (matrix - matrix * eye)) * inverse[c])
        left_one.append(left(one[c]))
    two = [times(left_one[c], right(one[c])) for c in every]
    base = [times(left_one[c], right(loads[c]())) for c in every]
    left_two = [left(two[c]) for c in every]
    pair = [times(left_two[c], right(one[c] + pltpu.roll(two[c], 64, 1))) for c in every]
    three = [jnp.where(lane < species_count, pair[c], 0.0) for c in every]
    four = [jnp.where(lane < species_count, pltpu.roll(pair[c], 64, 1), 0.0) for c in every]
    five = [times(left_two[c], right(three[c])) for c in every]
    left_five = [left(five[c]) for c in every]
    rest = []
    for c in every:
        more = [(counts[c] > q).astype(single) for q in (5, 6, 7, 8, 9)]
        rest.append(
            eye * more[0] + one[c] * more[1] + two[c] * more[2] + three[c] * more[3] + four[c] * more[4]
        )
    high_part = [times(left_five[c], right(rest[c])) for c in every]
    left_sum = [left(eye + one[c] + two[c] + three[c] + four[c] + high_part[c]) for c in every]
    base = [(base[c] + (inverse[c] - 1.0) * loads[c]()) * (1.0 / gamma) for c in every]
    first = []
    for c in every:
        values = loads[c]()
        first.append(base[c] - (inverse[c] * loss) * (values * values))
    first = [times(left_sum[c], right(first[c])) for c in every]
    moved = [times(left_one[c], right(first[c])) for c in every]
    second = []
    for c in every:
        shifted = loads[c]() + first[c]
        second.append(
            base[c]
            + (moved[c] + (inverse[c] - 1.0) * first[c]) * (1.0 / gamma)
            - (inverse[c] * loss) * (shifted * shifted)
            - (2.0 * inverse[c]) * first[c]
        )
    second = [times(left_sum[c], right(second[c])) for c in every]
    return [loads[c]() + 1.5 * first[c] + 0.5 * second[c] for c in every]


def react_kernel(first_row, rows, columns, at_once, counts_ref, x_ref, a_ref, loss_ref, mats, store):
    mats[...] = jnp.zeros_like(mats)
    total = len(rows)
    for r in range(total):
        for h in range(2):
            for i in range(species_count):
                mats[r * 2 + h, 8 * i : 8 * i + 8, 0:species_count] = a_ref[
                    r, 8 * h : 8 * h + 8, species_count * i : species_count * i + species_count
                ]
    row = lax.broadcasted_iota(jnp.int32, (species_count, species_count), 0)
    lane = lax.broadcasted_iota(jnp.int32, (species_count, species_count), 1)
    loss = jnp.sum(jnp.where(row == lane, loss_ref[...], 0.0), axis=1, keepdims=True)
    flat = x_ref.reshape(species_count * total * 16, depth)
    cells = [(r, y) for r in rows for y in columns]
    for start in range(0, len(cells), at_once):
        span = cells[start : start + at_once]
        results = react_columns(
            [(lambda r=r, y=y: flat[pl.ds(16 * r + y, species_count, 16 * total), :]) for r, y in span],
            [(lambda r=r, y=y: mats[2 * r + y // 8, pl.ds(y % 8, species_count, 8), :]) for r, y in span],
            loss,
            [counts_ref[first_row + r, y] for r, y in span],
        )
        for (r, y), result in zip(span, results):
            store(r, y, result)


def react_call(body, name, grid, rows, block, extra_specs, shapes, operands, limit=vmem):
    spec = pltpu.PrefetchScalarGridSpec(
        num_scalar_prefetch=1,
        grid=(grid,),
        in_specs=[
            pl.BlockSpec((species_count, rows, 16, depth), lambda g, _: (0, block(g), 0, 0)),
            pl.BlockSpec((rows, 16, species_count**2), lambda g, _: (block(g), 0, 0)),
            pl.BlockSpec((1, species_count), lambda g, _: (0, 0)),
            *extra_specs,
        ],
        out_specs=[pl.BlockSpec(s, lambda g, _: (0, 0, 0)) for s in shapes],
        scratch_shapes=[pltpu.VMEM((2 * rows, 8 * species_count, depth), single)],
    )
    return pl.pallas_call(
        body,
        out_shape=[jax.ShapeDtypeStruct(s, single) for s in shapes],
        grid_spec=spec,
        compiler_params=pltpu.CompilerParams(vmem_limit_bytes=limit),
        name=name,
    )(*operands)


def react_edges(species, matrices, loss, sweeps, flow_rows, flow_columns):
    def body(counts_ref, x_ref, a_ref, loss_ref, fr_ref, fc_ref, to_left, to_right, mats):
        g = pl.program_id(0)

        def store(r, y, result):
            target, column = (to_left, y) if y < 2 else (to_right, y - 14)
            target[2 * (4 * g + r) + column] = result

        react_kernel(4 * g, range(4), (0, 1, 14, 15), 16, counts_ref, x_ref, a_ref, loss_ref, mats, store)
        for target, column in ((to_left, 0), (to_right, 14)):
            for k, flow in enumerate((fr_ref, fc_ref)):
                for r in range(8):
                    target[16 + k, 2 * r : 2 * r + 2, :] = flow[r, column : column + 2, :]

    flow = pl.BlockSpec((8, 16, depth), lambda g, _: (0, 0, 0))
    shape = (18, species_count, depth)
    return react_call(
        body, "react_edges", 2, 4, lambda g: g, [flow, flow], [shape, shape],
        (sweeps, species, matrices, loss, flow_rows, flow_columns),
    )


def react_pair(pair, species, matrices, loss, sweeps, to_left, to_right):
    def body(counts_ref, x_ref, a_ref, loss_ref, left_ref, right_ref, o_ref, mats):
        def store(r, y, result):
            o_ref[16 * r + y] = result

        react_kernel(2 * pair, range(2), range(2, 14), 12, counts_ref, x_ref, a_ref, loss_ref, mats, store)
        for r in range(2):
            for y in range(2):
                o_ref[16 * r + y] = left_ref[2 * r + y]
                o_ref[16 * r + 14 + y] = right_ref[2 * r + y]

    edge = pl.BlockSpec((2 * 2, species_count, depth), lambda g, _: (pair, 0, 0))
    return react_call(
        body, f"react_pair_{pair}", 1, 2, lambda g: pair, [edge, edge], [(36, species_count, depth)],
        (sweeps, species, matrices, loss, to_left, to_right),
    )[0]


def react_middle(species, matrices, loss, sweeps):
    def body(counts_ref, x_ref, a_ref, loss_ref, o_ref, mats):
        g = pl.program_id(0)

        def store(r, y, result):
            o_ref[12 * (2 * g + r) + y - 2] = result

        react_kernel(2 + 2 * g, range(2), range(2, 14), 12, counts_ref, x_ref, a_ref, loss_ref, mats, store)

    return react_call(
        body, "react_middle", 2, 2, lambda g: 1 + g, [], [(48, species_count, depth)],
        (sweeps, species, matrices, loss),
    )[0]


def corner_kernel(low_in, high_in, before, after, fr_ref, fc_ref, low, high, flows, sems):
    copies = []

    def copy(source, target):
        k = len(copies)
        copies.append(pltpu.make_async_copy(source, target, sems.at[k]))
        copies[-1].start()

    for target, x in ((low, 0), (high, 7)):
        copy(before.at[pl.ds(2 * x + 1, 1)], target.at[pl.ds(32, 1)])
        copy(after.at[pl.ds(2 * x, 1)], target.at[pl.ds(33, 1)])
    flows[...] = jnp.zeros_like(flows)
    for t, (first, x) in enumerate(((0, 0), (6, 7))):
        for k, flow in enumerate((fr_ref, fc_ref)):
            for r in range(2):
                flows[t, k, 16 * r : 16 * r + 16, :] = flow[first + r]
            flows[t, k, 32:33, :] = before[16 + k, 2 * x + 1 : 2 * x + 2, :]
            flows[t, k, 33:34, :] = after[16 + k, 2 * x : 2 * x + 1, :]
    copy(flows.at[0], low.at[pl.ds(34, 2)])
    copy(flows.at[1], high.at[pl.ds(34, 2)])
    for one in copies:
        one.wait()


def add_corners(low, high, before, after, flow_rows, flow_columns):
    inside = pl.BlockSpec(memory_space=pltpu.VMEM)
    outside = pl.BlockSpec(memory_space=pl.ANY)
    shape = jax.ShapeDtypeStruct(low.shape, single)
    return pl.pallas_call(
        corner_kernel,
        out_shape=[shape, shape],
        in_specs=[outside, outside, inside, inside, inside, inside],
        out_specs=[outside, outside],
        input_output_aliases={0: 0, 1: 1},
        scratch_shapes=[pltpu.VMEM((2, 2, species_count, depth), single), pltpu.SemaphoreType.DMA((6,))],
        compiler_params=pltpu.CompilerParams(vmem_limit_bytes=vmem),
        name="add_corners",
    )(low, high, before, after, flow_rows, flow_columns)


def fill_weights(rows, has, weights, wide_rows, wide_columns):
    column = lax.broadcasted_iota(jnp.int32, (18, depth), 0)
    for i in rows:
        rows_out, rows_in = wide_rows[i + 2, 1:19, :], wide_rows[i + 1, 1:19, :]
        columns_out, columns_in = wide_columns[i + 2, 1:19, :], wide_columns[i + 2, 0:18, :]
        kept = jnp.where(column == 0, has[2], jnp.where(column == 17, has[3], 1.0))
        if i == -1:
            kept = kept * has[0]
        if i == 8:
            kept = kept * has[1]
        outward = (
            jnp.maximum(rows_out, 0.0)
            - jnp.minimum(rows_in, 0.0)
            + jnp.maximum(columns_out, 0.0)
            - jnp.minimum(columns_in, 0.0)
        )
        for q, weight in enumerate(
            (
                1.0 - outward,
                jnp.maximum(rows_in, 0.0),
                -jnp.minimum(rows_out, 0.0),
                jnp.maximum(columns_in, 0.0),
                -jnp.minimum(columns_out, 0.0),
            )
        ):
            weights[q, i + 1, 0:18, :] = kept * weight


def fill_inner(wide_rows, wide_columns, fr_ref, fc_ref, before, after):
    for k, (wide, own) in enumerate(((wide_rows, fr_ref), (wide_columns, fc_ref))):
        for r in range(8):
            wide[2 + r, 2:18, :] = own[r]
            wide[2 + r, 0:2, :] = before[16 + k, 2 * r : 2 * r + 2, :]
            wide[2 + r, 18:20, :] = after[16 + k, 2 * r : 2 * r + 2, :]


def move(source, weights, i, j):
    a = [weights[q, i + 1, j + 1 : j + 2, :] for q in range(5)]
    return (
        a[0] * source(i, j)
        + a[1] * source(i - 1, j)
        + a[2] * source(i + 1, j)
        + a[3] * source(i, j - 1)
        + a[4] * source(i, j + 1)
    )


def inner_kernel(
    inside_ref, low, middle, high, to_left, to_right, before, after, fr_ref, fc_ref,
    out, later, rows_out, wide_rows, wide_columns, weights, sems,
):
    fill_inner(wide_rows, wide_columns, fr_ref, fc_ref, before, after)
    fill_weights(range(1, 7), [inside_ref[q].astype(single) for q in range(4)], weights, wide_rows, wide_columns)

    def now(i, j):
        if j < 0:
            return before[2 * i + j + 2]
        if j > 15:
            return after[2 * i + j - 16]
        if i < 2:
            return low[16 * i + j]
        if i > 5:
            return high[16 * (i - 6) + j]
        if j < 2:
            return to_left[2 * i + j]
        if j > 13:
            return to_right[2 * i + j - 14]
        return middle[12 * (i - 2) + j - 2]

    copies = []
    for i in range(1, 7):
        for j in range(-1, 17):
            later[i - 1, j + 1] = move(now, weights, i, j)
        if i >= 3:
            x = i - 1
            flat = rows_out.at[x - 2].reshape(species_count * 16, depth)
            for j in range(16):
                flat[pl.ds(j, species_count, 16), :] = move(
                    lambda a, b: later[a - 1, b + 1], weights, x, j
                )
            copies.append(pltpu.make_async_copy(rows_out.at[x - 2], out.at[:, x], sems.at[x - 2]))
            copies[-1].start()
    for one in copies:
        one.wait()


def outer_kernel(
    inside_ref, done, inner, low, high, above, below, before, after, fr_ref, fc_ref,
    out, later, rows_out, wide_rows, wide_columns, weights, sems,
):
    fill_inner(wide_rows, wide_columns, fr_ref, fc_ref, before, after)
    for k, wide in enumerate((wide_rows, wide_columns)):
        for part, place in ((above, 0), (below, 10)):
            for r in range(2):
                wide[place + r, 2:18, :] = part[34 + k, 16 * r : 16 * r + 16, :]
        for part, place in ((above, 1), (below, 10)):
            wide[place, 1:2, :] = part[34 + k, 32:33, :]
            wide[place, 18:19, :] = part[34 + k, 33:34, :]
    rows = (-1, 0, 1, 6, 7, 8)
    fill_weights(rows, [inside_ref[q].astype(single) for q in range(4)], weights, wide_rows, wide_columns)

    def now(i, j):
        if i < 0 or i > 7:
            part, r = (above, i + 2) if i < 0 else (below, i - 8)
            if j < 0:
                return part[32]
            if j > 15:
                return part[33]
            return part[16 * r + j]
        if j < 0:
            return before[2 * i + j + 2]
        if j > 15:
            return after[2 * i + j - 16]
        return low[16 * i + j] if i < 2 else high[16 * (i - 6) + j]

    def soon(i, j):
        return inner[i - 1, j + 1] if 0 < i < 7 else later[{-1: 0, 0: 1, 7: 2, 8: 3}[i], j + 1]

    for q, i in enumerate((-1, 0, 7, 8)):
        for j in range(0, 16) if i in (-1, 8) else range(-1, 17):
            later[q, j + 1] = move(now, weights, i, j)
    copies = []
    for q, x in enumerate((0, 1, 6, 7)):
        flat = rows_out.at[q].reshape(species_count * 16, depth)
        for j in range(16):
            flat[pl.ds(j, species_count, 16), :] = move(soon, weights, x, j)
        copies.append(pltpu.make_async_copy(rows_out.at[q], out.at[:, x], sems.at[q]))
        copies[-1].start()
    for one in copies:
        one.wait()


def moved_call(body, name, inputs, shapes, specs, places, aliases):
    inside = pl.BlockSpec(memory_space=pltpu.VMEM)
    return pl.pallas_call(
        body,
        out_shape=shapes,
        in_specs=[pl.BlockSpec(memory_space=pltpu.SMEM)] + [
            pl.BlockSpec(memory_space=pl.ANY) if k in aliases else inside for k in range(1, len(inputs))
        ],
        out_specs=specs,
        input_output_aliases=aliases,
        scratch_shapes=[
            *places,
            pltpu.VMEM((4, species_count, 16, depth), single),
            pltpu.VMEM((12, 24, depth), single),
            pltpu.VMEM((12, 24, depth), single),
            pltpu.VMEM((5, 10, 24, depth), single),
            pltpu.SemaphoreType.DMA((4,)),
        ],
        compiler_params=pltpu.CompilerParams(vmem_limit_bytes=vmem_small),
        name=name,
    )(*inputs)


def transport(inside, low, middle, high, to_left, to_right, above, below, before, after, flow_rows, flow_columns):
    whole = jax.ShapeDtypeStruct((species_count, rows_here, columns_here, depth), single)
    outside = pl.BlockSpec(memory_space=pl.ANY)
    done, inner = moved_call(
        inner_kernel, "inner",
        (inside, low, middle, high, to_left, to_right, before, after, flow_rows, flow_columns),
        [whole, jax.ShapeDtypeStruct((6, 18, species_count, depth), single)],
        [outside, pl.BlockSpec(memory_space=pltpu.VMEM)], [], {},
    )
    return moved_call(
        outer_kernel, "outer",
        (inside, done, inner, low, high, above, below, before, after, flow_rows, flow_columns),
        whole, outside, [pltpu.VMEM((4, 18, species_count, depth), single)], {1: 0},
    )


def onward(array, axis, by):
    length = lax.axis_size(axis)
    pairs = [(i, i + by) for i in range(length) if 0 <= i + by < length]
    return lax.ppermute(array, axis, pairs)


def on_device(species, rate_matrices, loss_rates, sweeps, flow_rows, flow_columns):
    loss = loss_rates.reshape(1, species_count)
    arguments = (species, rate_matrices, loss, sweeps)
    kept = [pltpu.with_memory_space_constraint(a, pltpu.HBM) for a in (*arguments, flow_rows, flow_columns)]
    to_left, to_right = react_edges(*kept)
    before = onward(to_right, "gy", 1)
    after = onward(to_left, "gy", -1)
    high = react_pair(3, *arguments, to_left, to_right)
    low = react_pair(0, *arguments, to_left, to_right)
    low, high = add_corners(low, high, before, after, flow_rows, flow_columns)
    above = onward(high, "gx", 1)
    below = onward(low, "gx", -1)
    middle = react_middle(*arguments)
    x, y = lax.axis_index("gx"), lax.axis_index("gy")
    inside = jnp.stack(
        [x > 0, x < lax.axis_size("gx") - 1, y > 0, y < lax.axis_size("gy") - 1]
    ).astype(jnp.int32)
    return transport(
        inside, low, middle, high, to_left, to_right, above, below, before, after, flow_rows, flow_columns
    )


def solution(mesh):
    placed = (
        P(None, "gx", "gy", None),
        P("gx", "gy", None),
        P(),
        P("gx", "gy"),
        P("gx", "gy", None),
        P("gx", "gy", None),
    )
    return jax.shard_map(
        on_device, mesh=mesh, in_specs=placed, out_specs=P(None, "gx", "gy", None), check_vma=False
    )
```

```python
import jax
import jax.numpy as jnp
from jax import lax
from jax.experimental import pallas as pl
from jax.experimental.pallas import tpu as pltpu
from jax.sharding import PartitionSpec as P

gamma = 1.0 + 0.5**0.5
species_count = 48
depth = 128
rows_here = 8
columns_here = 16
single = jnp.float32
half = jnp.bfloat16
vmem = 40 << 20
vmem_small = 16 << 20


def left(matrix):
    high = matrix.astype(half).astype(single)
    lane = lax.broadcasted_iota(jnp.int32, (species_count, depth), 1)
    again = pltpu.roll(high, 96, 1)
    first = jnp.where(lane < 96, high + pltpu.roll(matrix - high, 48, 1), again).astype(half)
    return jnp.concatenate([first, again.astype(half)[:, :16]], axis=1)


def right(values):
    high = values.astype(half)
    low = (values - high.astype(single)).astype(half)
    return jnp.concatenate([high, high, low], axis=0)


def times(one, other):
    return jnp.dot(one, other, preferred_element_type=single)


def react_columns(loads, coefficients, loss, counts):
    every = range(len(loads))
    row = lax.broadcasted_iota(jnp.int32, (species_count, depth), 0)
    lane = lax.broadcasted_iota(jnp.int32, (species_count, depth), 1)
    eye = (row == lane).astype(single)
    inverse, one, left_one = [], [], []
    for c in every:
        matrix = coefficients[c]()
        scaled = 1.0 - gamma * jnp.sum(matrix * eye, axis=1, keepdims=True)
        inverse.append(1.0 / scaled)
        one.append((gamma * (matrix - matrix * eye)) * inverse[c])
        left_one.append(left(one[c]))
    two = [times(left_one[c], right(one[c])) for c in every]
    base = [times(left_one[c], right(loads[c]())) for c in every]
    left_two = [left(two[c]) for c in every]
    pair = [times(left_two[c], right(one[c] + pltpu.roll(two[c], 64, 1))) for c in every]
    three = [jnp.where(lane < species_count, pair[c], 0.0) for c in every]
    four = [jnp.where(lane < species_count, pltpu.roll(pair[c], 64, 1), 0.0) for c in every]
    five = [times(left_two[c], right(three[c])) for c in every]
    left_five = [left(five[c]) for c in every]
    rest = []
    for c in every:
        more = [(counts[c] > q).astype(single) for q in (5, 6, 7, 8, 9)]
        rest.append(
            eye * more[0] + one[c] * more[1] + two[c] * more[2] + three[c] * more[3] + four[c] * more[4]
        )
    high_part = [times(left_five[c], right(rest[c])) for c in every]
    left_sum = [left(eye + one[c] + two[c] + three[c] + four[c] + high_part[c]) for c in every]
    base = [(base[c] + (inverse[c] - 1.0) * loads[c]()) * (1.0 / gamma) for c in every]
    first = []
    for c in every:
        values = loads[c]()
        first.append(base[c] - (inverse[c] * loss) * (values * values))
    first = [times(left_sum[c], right(first[c])) for c in every]
    moved = [times(left_one[c], right(first[c])) for c in every]
    second = []
    for c in every:
        shifted = loads[c]() + first[c]
        second.append(
            base[c]
            + (moved[c] + (inverse[c] - 1.0) * first[c]) * (1.0 / gamma)
            - (inverse[c] * loss) * (shifted * shifted)
            - (2.0 * inverse[c]) * first[c]
        )
    second = [times(left_sum[c], right(second[c])) for c in every]
    return [loads[c]() + 1.5 * first[c] + 0.5 * second[c] for c in every]


def react_kernel(parts, rows, columns, at_once, counts_ref, loss_ref, mats, store):
    mats[...] = jnp.zeros_like(mats)
    total = len(rows)
    for p, (_, _, a_ref) in enumerate(parts):
        for r in range(total):
            for h in range(2):
                for i in range(species_count):
                    mats[2 * (p * total + r) + h, 8 * i : 8 * i + 8, 0:species_count] = a_ref[
                        r, 8 * h : 8 * h + 8, species_count * i : species_count * i + species_count
                    ]
    row = lax.broadcasted_iota(jnp.int32, (species_count, species_count), 0)
    lane = lax.broadcasted_iota(jnp.int32, (species_count, species_count), 1)
    loss = jnp.sum(jnp.where(row == lane, loss_ref[...], 0.0), axis=1, keepdims=True)
    flat = [x_ref.reshape(species_count * total * 16, depth) for _, x_ref, _ in parts]
    cells = [(p, r, y) for p in range(len(parts)) for r in rows for y in columns]
    for start in range(0, len(cells), at_once):
        span = cells[start : start + at_once]
        results = react_columns(
            [
                (lambda p=p, r=r, y=y: flat[p][pl.ds(16 * r + y, species_count, 16 * total), :])
                for p, r, y in span
            ],
            [
                (lambda p=p, r=r, y=y: mats[2 * (p * total + r) + y // 8, pl.ds(y % 8, species_count, 8), :])
                for p, r, y in span
            ],
            loss,
            [counts_ref[parts[p][0] + r, y] for p, r, y in span],
        )
        for (p, r, y), result in zip(span, results):
            store(p, r, y, result)


def react_call(body, name, grid, rows, blocks, extra_specs, shapes, operands):
    parts = []
    for block in blocks:
        parts.append(pl.BlockSpec((species_count, rows, 16, depth), lambda g, _, b=block: (0, b(g), 0, 0)))
        parts.append(pl.BlockSpec((rows, 16, species_count**2), lambda g, _, b=block: (b(g), 0, 0)))
    spec = pltpu.PrefetchScalarGridSpec(
        num_scalar_prefetch=1,
        grid=(grid,),
        in_specs=[pl.BlockSpec((1, species_count), lambda g, _: (0, 0)), *parts, *extra_specs],
        out_specs=[pl.BlockSpec(s, lambda g, _: (0, 0, 0)) for s in shapes],
        scratch_shapes=[pltpu.VMEM((2 * rows * len(blocks), 8 * species_count, depth), single)],
    )
    return pl.pallas_call(
        body,
        out_shape=[jax.ShapeDtypeStruct(s, single) for s in shapes],
        grid_spec=spec,
        compiler_params=pltpu.CompilerParams(vmem_limit_bytes=vmem),
        name=name,
    )(*operands)


def react_edges(species, matrices, loss, sweeps, flow_rows, flow_columns):
    def body(counts_ref, loss_ref, x_ref, a_ref, fr_ref, fc_ref, to_left, to_right, mats):
        g = pl.program_id(0)

        def store(_, r, y, result):
            target, column = (to_left, y) if y < 2 else (to_right, y - 14)
            target[2 * (4 * g + r) + column] = result

        react_kernel(
            [(4 * g, x_ref, a_ref)], range(4), (0, 1, 14, 15), 16, counts_ref, loss_ref, mats, store
        )
        for target, column in ((to_left, 0), (to_right, 14)):
            for k, flow in enumerate((fr_ref, fc_ref)):
                for r in range(8):
                    target[16 + k, 2 * r : 2 * r + 2, :] = flow[r, column : column + 2, :]

    flow = pl.BlockSpec((8, 16, depth), lambda g, _: (0, 0, 0))
    shape = (18, species_count, depth)
    return react_call(
        body, "react_edges", 2, 4, [lambda g: g], [flow, flow], [shape, shape],
        (sweeps, loss, species, matrices, flow_rows, flow_columns),
    )


def react_ends(species, matrices, loss, sweeps, to_left, to_right):
    def body(counts_ref, loss_ref, x_low, a_low, x_high, a_high, l_low, r_low, l_high, r_high, low, high, mats):
        ends = (low, high)

        def store(p, r, y, result):
            ends[p][16 * r + y] = result

        react_kernel(
            [(0, x_low, a_low), (6, x_high, a_high)],
            range(2), range(2, 14), 16, counts_ref, loss_ref, mats, store,
        )
        for target, left_ref, right_ref in ((low, l_low, r_low), (high, l_high, r_high)):
            for r in range(2):
                for y in range(2):
                    target[16 * r + y] = left_ref[2 * r + y]
                    target[16 * r + 14 + y] = right_ref[2 * r + y]

    edges = [pl.BlockSpec((4, species_count, depth), lambda g, _, b=b: (b, 0, 0)) for b in (0, 3)]
    return react_call(
        body, "react_ends", 1, 2, [lambda g: 0, lambda g: 3], [edges[0], edges[0], edges[1], edges[1]],
        [(36, species_count, depth)] * 2,
        (sweeps, loss, species, matrices, species, matrices, to_left, to_right, to_left, to_right),
    )


def react_middle(species, matrices, loss, sweeps):
    def body(counts_ref, loss_ref, x_ref, a_ref, o_ref, mats):
        g = pl.program_id(0)

        def store(_, r, y, result):
            o_ref[12 * (2 * g + r) + y - 2] = result

        react_kernel(
            [(2 + 2 * g, x_ref, a_ref)], range(2), range(2, 14), 12, counts_ref, loss_ref, mats, store
        )

    return react_call(
        body, "react_middle", 2, 2, [lambda g: 1 + g], [], [(48, species_count, depth)],
        (sweeps, loss, species, matrices),
    )[0]


def corner_kernel(low_in, high_in, before, after, fr_ref, fc_ref, low, high, flows, sems):
    copies = []

    def copy(source, target):
        k = len(copies)
        copies.append(pltpu.make_async_copy(source, target, sems.at[k]))
        copies[-1].start()

    for target, x in ((low, 0), (high, 7)):
        copy(before.at[pl.ds(2 * x + 1, 1)], target.at[pl.ds(32, 1)])
        copy(after.at[pl.ds(2 * x, 1)], target.at[pl.ds(33, 1)])
    flows[...] = jnp.zeros_like(flows)
    for t, (first, x) in enumerate(((0, 0), (6, 7))):
        for k, flow in enumerate((fr_ref, fc_ref)):
            for r in range(2):
                flows[t, k, 16 * r : 16 * r + 16, :] = flow[first + r]
            flows[t, k, 32:33, :] = before[16 + k, 2 * x + 1 : 2 * x + 2, :]
            flows[t, k, 33:34, :] = after[16 + k, 2 * x : 2 * x + 1, :]
    copy(flows.at[0], low.at[pl.ds(34, 2)])
    copy(flows.at[1], high.at[pl.ds(34, 2)])
    for one in copies:
        one.wait()


def add_corners(low, high, before, after, flow_rows, flow_columns):
    inside = pl.BlockSpec(memory_space=pltpu.VMEM)
    outside = pl.BlockSpec(memory_space=pl.ANY)
    shape = jax.ShapeDtypeStruct(low.shape, single)
    return pl.pallas_call(
        corner_kernel,
        out_shape=[shape, shape],
        in_specs=[outside, outside, inside, inside, inside, inside],
        out_specs=[outside, outside],
        input_output_aliases={0: 0, 1: 1},
        scratch_shapes=[pltpu.VMEM((2, 2, species_count, depth), single), pltpu.SemaphoreType.DMA((6,))],
        compiler_params=pltpu.CompilerParams(vmem_limit_bytes=vmem),
        name="add_corners",
    )(low, high, before, after, flow_rows, flow_columns)


def fill_weights(rows, has, weights, wide_rows, wide_columns):
    column = lax.broadcasted_iota(jnp.int32, (18, depth), 0)
    for i in rows:
        rows_out, rows_in = wide_rows[i + 2, 1:19, :], wide_rows[i + 1, 1:19, :]
        columns_out, columns_in = wide_columns[i + 2, 1:19, :], wide_columns[i + 2, 0:18, :]
        kept = jnp.where(column == 0, has[2], jnp.where(column == 17, has[3], 1.0))
        if i == -1:
            kept = kept * has[0]
        if i == 8:
            kept = kept * has[1]
        outward = (
            jnp.maximum(rows_out, 0.0)
            - jnp.minimum(rows_in, 0.0)
            + jnp.maximum(columns_out, 0.0)
            - jnp.minimum(columns_in, 0.0)
        )
        for q, weight in enumerate(
            (
                1.0 - outward,
                jnp.maximum(rows_in, 0.0),
                -jnp.minimum(rows_out, 0.0),
                jnp.maximum(columns_in, 0.0),
                -jnp.minimum(columns_out, 0.0),
            )
        ):
            weights[q, i + 1, 0:18, :] = kept * weight


def fill_inner(wide_rows, wide_columns, fr_ref, fc_ref, before, after):
    for k, (wide, own) in enumerate(((wide_rows, fr_ref), (wide_columns, fc_ref))):
        for r in range(8):
            wide[2 + r, 2:18, :] = own[r]
            wide[2 + r, 0:2, :] = before[16 + k, 2 * r : 2 * r + 2, :]
            wide[2 + r, 18:20, :] = after[16 + k, 2 * r : 2 * r + 2, :]


def move(source, weights, i, j):
    a = [weights[q, i + 1, j + 1 : j + 2, :] for q in range(5)]
    return (
        a[0] * source(i, j)
        + a[1] * source(i - 1, j)
        + a[2] * source(i + 1, j)
        + a[3] * source(i, j - 1)
        + a[4] * source(i, j + 1)
    )


def inner_kernel(
    inside_ref, low, middle, high, to_left, to_right, before, after, fr_ref, fc_ref,
    out, later, rows_out, wide_rows, wide_columns, weights, sems,
):
    fill_inner(wide_rows, wide_columns, fr_ref, fc_ref, before, after)
    fill_weights(range(1, 7), [inside_ref[q].astype(single) for q in range(4)], weights, wide_rows, wide_columns)

    def now(i, j):
        if j < 0:
            return before[2 * i + j + 2]
        if j > 15:
            return after[2 * i + j - 16]
        if i < 2:
            return low[16 * i + j]
        if i > 5:
            return high[16 * (i - 6) + j]
        if j < 2:
            return to_left[2 * i + j]
        if j > 13:
            return to_right[2 * i + j - 14]
        return middle[12 * (i - 2) + j - 2]

    copies = []
    for i in range(1, 7):
        for j in range(-1, 17):
            later[i - 1, j + 1] = move(now, weights, i, j)
        if i >= 3:
            x = i - 1
            flat = rows_out.at[x - 2].reshape(species_count * 16, depth)
            for j in range(16):
                flat[pl.ds(j, species_count, 16), :] = move(
                    lambda a, b: later[a - 1, b + 1], weights, x, j
                )
            copies.append(pltpu.make_async_copy(rows_out.at[x - 2], out.at[:, x], sems.at[x - 2]))
            copies[-1].start()
    for one in copies:
        one.wait()


def outer_kernel(
    inside_ref, done, inner, low, high, above, below, before, after, fr_ref, fc_ref,
    out, later, rows_out, wide_rows, wide_columns, weights, sems,
):
    fill_inner(wide_rows, wide_columns, fr_ref, fc_ref, before, after)
    for k, wide in enumerate((wide_rows, wide_columns)):
        for part, place in ((above, 0), (below, 10)):
            for r in range(2):
                wide[place + r, 2:18, :] = part[34 + k, 16 * r : 16 * r + 16, :]
        for part, place in ((above, 1), (below, 10)):
            wide[place, 1:2, :] = part[34 + k, 32:33, :]
            wide[place, 18:19, :] = part[34 + k, 33:34, :]
    rows = (-1, 0, 1, 6, 7, 8)
    fill_weights(rows, [inside_ref[q].astype(single) for q in range(4)], weights, wide_rows, wide_columns)

    def now(i, j):
        if i < 0 or i > 7:
            part, r = (above, i + 2) if i < 0 else (below, i - 8)
            if j < 0:
                return part[32]
            if j > 15:
                return part[33]
            return part[16 * r + j]
        if j < 0:
            return before[2 * i + j + 2]
        if j > 15:
            return after[2 * i + j - 16]
        return low[16 * i + j] if i < 2 else high[16 * (i - 6) + j]

    def soon(i, j):
        return inner[i - 1, j + 1] if 0 < i < 7 else later[{-1: 0, 0: 1, 7: 2, 8: 3}[i], j + 1]

    for q, i in enumerate((-1, 0, 7, 8)):
        for j in range(0, 16) if i in (-1, 8) else range(-1, 17):
            later[q, j + 1] = move(now, weights, i, j)
    copies = []
    for q, x in enumerate((0, 1, 6, 7)):
        flat = rows_out.at[q].reshape(species_count * 16, depth)
        for j in range(16):
            flat[pl.ds(j, species_count, 16), :] = move(soon, weights, x, j)
        copies.append(pltpu.make_async_copy(rows_out.at[q], out.at[:, x], sems.at[q]))
        copies[-1].start()
    for one in copies:
        one.wait()


def moved_call(body, name, inputs, shapes, specs, places, aliases):
    inside = pl.BlockSpec(memory_space=pltpu.VMEM)
    return pl.pallas_call(
        body,
        out_shape=shapes,
        in_specs=[pl.BlockSpec(memory_space=pltpu.SMEM)] + [
            pl.BlockSpec(memory_space=pl.ANY) if k in aliases else inside for k in range(1, len(inputs))
        ],
        out_specs=specs,
        input_output_aliases=aliases,
        scratch_shapes=[
            *places,
            pltpu.VMEM((4, species_count, 16, depth), single),
            pltpu.VMEM((12, 24, depth), single),
            pltpu.VMEM((12, 24, depth), single),
            pltpu.VMEM((5, 10, 24, depth), single),
            pltpu.SemaphoreType.DMA((4,)),
        ],
        compiler_params=pltpu.CompilerParams(vmem_limit_bytes=vmem_small),
        name=name,
    )(*inputs)


def transport(inside, low, middle, high, to_left, to_right, above, below, before, after, flow_rows, flow_columns):
    whole = jax.ShapeDtypeStruct((species_count, rows_here, columns_here, depth), single)
    outside = pl.BlockSpec(memory_space=pl.ANY)
    done, inner = moved_call(
        inner_kernel, "inner",
        (inside, low, middle, high, to_left, to_right, before, after, flow_rows, flow_columns),
        [whole, jax.ShapeDtypeStruct((6, 18, species_count, depth), single)],
        [outside, pl.BlockSpec(memory_space=pltpu.VMEM)], [], {},
    )
    return moved_call(
        outer_kernel, "outer",
        (inside, done, inner, low, high, above, below, before, after, flow_rows, flow_columns),
        whole, outside, [pltpu.VMEM((4, 18, species_count, depth), single)], {1: 0},
    )


def onward(array, axis, by):
    length = lax.axis_size(axis)
    pairs = [(i, i + by) for i in range(length) if 0 <= i + by < length]
    return lax.ppermute(array, axis, pairs)


def on_device(species, rate_matrices, loss_rates, sweeps, flow_rows, flow_columns):
    loss = loss_rates.reshape(1, species_count)
    arguments = (species, rate_matrices, loss, sweeps)
    kept = [pltpu.with_memory_space_constraint(a, pltpu.HBM) for a in (*arguments, flow_rows, flow_columns)]
    to_left, to_right = react_edges(*kept)
    before = onward(to_right, "gy", 1)
    after = onward(to_left, "gy", -1)
    low, high = react_ends(*arguments, to_left, to_right)
    low, high = add_corners(low, high, before, after, flow_rows, flow_columns)
    above = onward(high, "gx", 1)
    below = onward(low, "gx", -1)
    middle = react_middle(*arguments)
    x, y = lax.axis_index("gx"), lax.axis_index("gy")
    inside = jnp.stack(
        [x > 0, x < lax.axis_size("gx") - 1, y > 0, y < lax.axis_size("gy") - 1]
    ).astype(jnp.int32)
    return transport(
        inside, low, middle, high, to_left, to_right, above, below, before, after, flow_rows, flow_columns
    )


def solution(mesh):
    placed = (
        P(None, "gx", "gy", None),
        P("gx", "gy", None),
        P(),
        P("gx", "gy"),
        P("gx", "gy", None),
        P("gx", "gy", None),
    )
    return jax.shard_map(
        on_device, mesh=mesh, in_specs=placed, out_specs=P(None, "gx", "gy", None), check_vma=False
    )
```

```python
import jax
import jax.numpy as jnp
from jax import lax
from jax.experimental import pallas as pl
from jax.experimental.pallas import tpu as pltpu
from jax.sharding import PartitionSpec as P

gamma = 1.0 + 0.5**0.5
species_count = 48
depth = 128
rows_here = 8
columns_here = 16
single = jnp.float32
half = jnp.bfloat16
vmem = 40 << 20
vmem_small = 16 << 20


def left(matrix):
    high = matrix.astype(half).astype(single)
    lane = lax.broadcasted_iota(jnp.int32, (species_count, depth), 1)
    again = pltpu.roll(high, 96, 1)
    first = jnp.where(lane < 96, high + pltpu.roll(matrix - high, 48, 1), again).astype(half)
    return jnp.concatenate([first, again.astype(half)[:, :16]], axis=1)


def right(values):
    high = values.astype(half)
    low = (values - high.astype(single)).astype(half)
    return jnp.concatenate([high, high, low], axis=0)


def times(one, other):
    return jnp.dot(one, other, preferred_element_type=single)


def react_columns(loads, coefficients, loss, counts):
    every = range(len(loads))
    row = lax.broadcasted_iota(jnp.int32, (species_count, depth), 0)
    lane = lax.broadcasted_iota(jnp.int32, (species_count, depth), 1)
    eye = (row == lane).astype(single)
    inverse, one, left_one = [], [], []
    for c in every:
        matrix = coefficients[c]()
        scaled = 1.0 - gamma * jnp.sum(matrix * eye, axis=1, keepdims=True)
        inverse.append(1.0 / scaled)
        one.append((gamma * (matrix - matrix * eye)) * inverse[c])
        left_one.append(left(one[c]))
    both = [times(left_one[c], right(jnp.concatenate([loads[c](), one[c]], axis=1))) for c in every]
    two = [pair[:, depth:] for pair in both]
    base = [pair[:, :depth] for pair in both]
    left_two = [left(two[c]) for c in every]
    pair = [times(left_two[c], right(one[c] + pltpu.roll(two[c], 64, 1))) for c in every]
    three = [jnp.where(lane < species_count, pair[c], 0.0) for c in every]
    four = [jnp.where(lane < species_count, pltpu.roll(pair[c], 64, 1), 0.0) for c in every]
    five = [times(left_two[c], right(three[c])) for c in every]
    left_five = [left(five[c]) for c in every]
    rest = []
    for c in every:
        more = [(counts[c] > q).astype(single) for q in (5, 6, 7, 8, 9)]
        rest.append(
            eye * more[0] + one[c] * more[1] + two[c] * more[2] + three[c] * more[3] + four[c] * more[4]
        )
    high_part = [times(left_five[c], right(rest[c])) for c in every]
    left_sum = [left(eye + one[c] + two[c] + three[c] + four[c] + high_part[c]) for c in every]
    base = [(base[c] + (inverse[c] - 1.0) * loads[c]()) * (1.0 / gamma) for c in every]
    first = []
    for c in every:
        values = loads[c]()
        first.append(base[c] - (inverse[c] * loss) * (values * values))
    first = [times(left_sum[c], right(first[c])) for c in every]
    moved = [times(left_one[c], right(first[c])) for c in every]
    second = []
    for c in every:
        shifted = loads[c]() + first[c]
        second.append(
            base[c]
            + (moved[c] + (inverse[c] - 1.0) * first[c]) * (1.0 / gamma)
            - (inverse[c] * loss) * (shifted * shifted)
            - (2.0 * inverse[c]) * first[c]
        )
    second = [times(left_sum[c], right(second[c])) for c in every]
    return [loads[c]() + 1.5 * first[c] + 0.5 * second[c] for c in every]


def react_kernel(parts, rows, columns, at_once, counts_ref, loss_ref, mats, store):
    mats[...] = jnp.zeros_like(mats)
    total = len(rows)
    for p, (_, _, a_ref) in enumerate(parts):
        for r in range(total):
            for h in range(2):
                for i in range(species_count):
                    mats[2 * (p * total + r) + h, 8 * i : 8 * i + 8, 0:species_count] = a_ref[
                        r, 8 * h : 8 * h + 8, species_count * i : species_count * i + species_count
                    ]
    row = lax.broadcasted_iota(jnp.int32, (species_count, species_count), 0)
    lane = lax.broadcasted_iota(jnp.int32, (species_count, species_count), 1)
    loss = jnp.sum(jnp.where(row == lane, loss_ref[...], 0.0), axis=1, keepdims=True)
    flat = [x_ref.reshape(species_count * total * 16, depth) for _, x_ref, _ in parts]
    cells = [(p, r, y) for p in range(len(parts)) for r in rows for y in columns]
    for start in range(0, len(cells), at_once):
        span = cells[start : start + at_once]
        results = react_columns(
            [
                (lambda p=p, r=r, y=y: flat[p][pl.ds(16 * r + y, species_count, 16 * total), :])
                for p, r, y in span
            ],
            [
                (lambda p=p, r=r, y=y: mats[2 * (p * total + r) + y // 8, pl.ds(y % 8, species_count, 8), :])
                for p, r, y in span
            ],
            loss,
            [counts_ref[parts[p][0] + r, y] for p, r, y in span],
        )
        for (p, r, y), result in zip(span, results):
            store(p, r, y, result)


def react_call(body, name, grid, rows, blocks, extra_specs, shapes, operands):
    parts = []
    for block in blocks:
        parts.append(pl.BlockSpec((species_count, rows, 16, depth), lambda g, _, b=block: (0, b(g), 0, 0)))
        parts.append(pl.BlockSpec((rows, 16, species_count**2), lambda g, _, b=block: (b(g), 0, 0)))
    spec = pltpu.PrefetchScalarGridSpec(
        num_scalar_prefetch=1,
        grid=(grid,),
        in_specs=[pl.BlockSpec((1, species_count), lambda g, _: (0, 0)), *parts, *extra_specs],
        out_specs=[pl.BlockSpec(s, lambda g, _: (0, 0, 0)) for s in shapes],
        scratch_shapes=[pltpu.VMEM((2 * rows * len(blocks), 8 * species_count, depth), single)],
    )
    return pl.pallas_call(
        body,
        out_shape=[jax.ShapeDtypeStruct(s, single) for s in shapes],
        grid_spec=spec,
        compiler_params=pltpu.CompilerParams(vmem_limit_bytes=vmem),
        name=name,
    )(*operands)


def react_edges(species, matrices, loss, sweeps, flow_rows, flow_columns):
    def body(counts_ref, loss_ref, x_ref, a_ref, fr_ref, fc_ref, to_left, to_right, mats):
        g = pl.program_id(0)

        def store(_, r, y, result):
            target, column = (to_left, y) if y < 2 else (to_right, y - 14)
            target[2 * (4 * g + r) + column] = result

        react_kernel(
            [(4 * g, x_ref, a_ref)], range(4), (0, 1, 14, 15), 16, counts_ref, loss_ref, mats, store
        )
        for target, column in ((to_left, 0), (to_right, 14)):
            for k, flow in enumerate((fr_ref, fc_ref)):
                for r in range(8):
                    target[16 + k, 2 * r : 2 * r + 2, :] = flow[r, column : column + 2, :]

    flow = pl.BlockSpec((8, 16, depth), lambda g, _: (0, 0, 0))
    shape = (18, species_count, depth)
    return react_call(
        body, "react_edges", 2, 4, [lambda g: g], [flow, flow], [shape, shape],
        (sweeps, loss, species, matrices, flow_rows, flow_columns),
    )


def react_ends(species, matrices, loss, sweeps, to_left, to_right):
    def body(counts_ref, loss_ref, x_low, a_low, x_high, a_high, l_low, r_low, l_high, r_high, low, high, mats):
        ends = (low, high)

        def store(p, r, y, result):
            ends[p][16 * r + y] = result

        react_kernel(
            [(0, x_low, a_low), (6, x_high, a_high)],
            range(2), range(2, 14), 16, counts_ref, loss_ref, mats, store,
        )
        for target, left_ref, right_ref in ((low, l_low, r_low), (high, l_high, r_high)):
            for r in range(2):
                for y in range(2):
                    target[16 * r + y] = left_ref[2 * r + y]
                    target[16 * r + 14 + y] = right_ref[2 * r + y]

    edges = [pl.BlockSpec((4, species_count, depth), lambda g, _, b=b: (b, 0, 0)) for b in (0, 3)]
    return react_call(
        body, "react_ends", 1, 2, [lambda g: 0, lambda g: 3], [edges[0], edges[0], edges[1], edges[1]],
        [(36, species_count, depth)] * 2,
        (sweeps, loss, species, matrices, species, matrices, to_left, to_right, to_left, to_right),
    )


def react_middle(species, matrices, loss, sweeps):
    def body(counts_ref, loss_ref, x_ref, a_ref, o_ref, mats):
        g = pl.program_id(0)

        def store(_, r, y, result):
            o_ref[12 * (2 * g + r) + y - 2] = result

        react_kernel(
            [(2 + 2 * g, x_ref, a_ref)], range(2), range(2, 14), 12, counts_ref, loss_ref, mats, store
        )

    return react_call(
        body, "react_middle", 2, 2, [lambda g: 1 + g], [], [(48, species_count, depth)],
        (sweeps, loss, species, matrices),
    )[0]


def corner_kernel(low_in, high_in, before, after, fr_ref, fc_ref, low, high, flows, sems):
    copies = []

    def copy(source, target):
        k = len(copies)
        copies.append(pltpu.make_async_copy(source, target, sems.at[k]))
        copies[-1].start()

    for target, x in ((low, 0), (high, 7)):
        copy(before.at[pl.ds(2 * x + 1, 1)], target.at[pl.ds(32, 1)])
        copy(after.at[pl.ds(2 * x, 1)], target.at[pl.ds(33, 1)])
    flows[...] = jnp.zeros_like(flows)
    for t, (first, x) in enumerate(((0, 0), (6, 7))):
        for k, flow in enumerate((fr_ref, fc_ref)):
            for r in range(2):
                flows[t, k, 16 * r : 16 * r + 16, :] = flow[first + r]
            flows[t, k, 32:33, :] = before[16 + k, 2 * x + 1 : 2 * x + 2, :]
            flows[t, k, 33:34, :] = after[16 + k, 2 * x : 2 * x + 1, :]
    copy(flows.at[0], low.at[pl.ds(34, 2)])
    copy(flows.at[1], high.at[pl.ds(34, 2)])
    for one in copies:
        one.wait()


def add_corners(low, high, before, after, flow_rows, flow_columns):
    inside = pl.BlockSpec(memory_space=pltpu.VMEM)
    outside = pl.BlockSpec(memory_space=pl.ANY)
    shape = jax.ShapeDtypeStruct(low.shape, single)
    return pl.pallas_call(
        corner_kernel,
        out_shape=[shape, shape],
        in_specs=[outside, outside, inside, inside, inside, inside],
        out_specs=[outside, outside],
        input_output_aliases={0: 0, 1: 1},
        scratch_shapes=[pltpu.VMEM((2, 2, species_count, depth), single), pltpu.SemaphoreType.DMA((6,))],
        compiler_params=pltpu.CompilerParams(vmem_limit_bytes=vmem),
        name="add_corners",
    )(low, high, before, after, flow_rows, flow_columns)


def fill_weights(rows, has, weights, wide_rows, wide_columns):
    column = lax.broadcasted_iota(jnp.int32, (18, depth), 0)
    for i in rows:
        rows_out, rows_in = wide_rows[i + 2, 1:19, :], wide_rows[i + 1, 1:19, :]
        columns_out, columns_in = wide_columns[i + 2, 1:19, :], wide_columns[i + 2, 0:18, :]
        kept = jnp.where(column == 0, has[2], jnp.where(column == 17, has[3], 1.0))
        if i == -1:
            kept = kept * has[0]
        if i == 8:
            kept = kept * has[1]
        outward = (
            jnp.maximum(rows_out, 0.0)
            - jnp.minimum(rows_in, 0.0)
            + jnp.maximum(columns_out, 0.0)
            - jnp.minimum(columns_in, 0.0)
        )
        for q, weight in enumerate(
            (
                1.0 - outward,
                jnp.maximum(rows_in, 0.0),
                -jnp.minimum(rows_out, 0.0),
                jnp.maximum(columns_in, 0.0),
                -jnp.minimum(columns_out, 0.0),
            )
        ):
            weights[q, i + 1, 0:18, :] = kept * weight


def fill_inner(wide_rows, wide_columns, fr_ref, fc_ref, before, after):
    for k, (wide, own) in enumerate(((wide_rows, fr_ref), (wide_columns, fc_ref))):
        for r in range(8):
            wide[2 + r, 2:18, :] = own[r]
            wide[2 + r, 0:2, :] = before[16 + k, 2 * r : 2 * r + 2, :]
            wide[2 + r, 18:20, :] = after[16 + k, 2 * r : 2 * r + 2, :]


def move(source, weights, i, j):
    a = [weights[q, i + 1, j + 1 : j + 2, :] for q in range(5)]
    return (
        a[0] * source(i, j)
        + a[1] * source(i - 1, j)
        + a[2] * source(i + 1, j)
        + a[3] * source(i, j - 1)
        + a[4] * source(i, j + 1)
    )


def inner_kernel(
    inside_ref, low, middle, high, to_left, to_right, before, after, fr_ref, fc_ref,
    out, later, rows_out, wide_rows, wide_columns, weights, sems,
):
    fill_inner(wide_rows, wide_columns, fr_ref, fc_ref, before, after)
    fill_weights(range(1, 7), [inside_ref[q].astype(single) for q in range(4)], weights, wide_rows, wide_columns)

    def now(i, j):
        if j < 0:
            return before[2 * i + j + 2]
        if j > 15:
            return after[2 * i + j - 16]
        if i < 2:
            return low[16 * i + j]
        if i > 5:
            return high[16 * (i - 6) + j]
        if j < 2:
            return to_left[2 * i + j]
        if j > 13:
            return to_right[2 * i + j - 14]
        return middle[12 * (i - 2) + j - 2]

    copies = []
    for i in range(1, 7):
        for j in range(-1, 17):
            later[i - 1, j + 1] = move(now, weights, i, j)
        if i >= 3:
            x = i - 1
            flat = rows_out.at[x - 2].reshape(species_count * 16, depth)
            for j in range(16):
                flat[pl.ds(j, species_count, 16), :] = move(
                    lambda a, b: later[a - 1, b + 1], weights, x, j
                )
            copies.append(pltpu.make_async_copy(rows_out.at[x - 2], out.at[:, x], sems.at[x - 2]))
            copies[-1].start()
    for one in copies:
        one.wait()


def outer_kernel(
    inside_ref, done, inner, low, high, above, below, before, after, fr_ref, fc_ref,
    out, later, rows_out, wide_rows, wide_columns, weights, sems,
):
    fill_inner(wide_rows, wide_columns, fr_ref, fc_ref, before, after)
    for k, wide in enumerate((wide_rows, wide_columns)):
        for part, place in ((above, 0), (below, 10)):
            for r in range(2):
                wide[place + r, 2:18, :] = part[34 + k, 16 * r : 16 * r + 16, :]
        for part, place in ((above, 1), (below, 10)):
            wide[place, 1:2, :] = part[34 + k, 32:33, :]
            wide[place, 18:19, :] = part[34 + k, 33:34, :]
    rows = (-1, 0, 1, 6, 7, 8)
    fill_weights(rows, [inside_ref[q].astype(single) for q in range(4)], weights, wide_rows, wide_columns)

    def now(i, j):
        if i < 0 or i > 7:
            part, r = (above, i + 2) if i < 0 else (below, i - 8)
            if j < 0:
                return part[32]
            if j > 15:
                return part[33]
            return part[16 * r + j]
        if j < 0:
            return before[2 * i + j + 2]
        if j > 15:
            return after[2 * i + j - 16]
        return low[16 * i + j] if i < 2 else high[16 * (i - 6) + j]

    def soon(i, j):
        return inner[i - 1, j + 1] if 0 < i < 7 else later[{-1: 0, 0: 1, 7: 2, 8: 3}[i], j + 1]

    for q, i in enumerate((-1, 0, 7, 8)):
        for j in range(0, 16) if i in (-1, 8) else range(-1, 17):
            later[q, j + 1] = move(now, weights, i, j)
    copies = []
    for q, x in enumerate((0, 1, 6, 7)):
        flat = rows_out.at[q].reshape(species_count * 16, depth)
        for j in range(16):
            flat[pl.ds(j, species_count, 16), :] = move(soon, weights, x, j)
        copies.append(pltpu.make_async_copy(rows_out.at[q], out.at[:, x], sems.at[q]))
        copies[-1].start()
    for one in copies:
        one.wait()


def moved_call(body, name, inputs, shapes, specs, places, aliases):
    inside = pl.BlockSpec(memory_space=pltpu.VMEM)
    return pl.pallas_call(
        body,
        out_shape=shapes,
        in_specs=[pl.BlockSpec(memory_space=pltpu.SMEM)] + [
            pl.BlockSpec(memory_space=pl.ANY) if k in aliases else inside for k in range(1, len(inputs))
        ],
        out_specs=specs,
        input_output_aliases=aliases,
        scratch_shapes=[
            *places,
            pltpu.VMEM((4, species_count, 16, depth), single),
            pltpu.VMEM((12, 24, depth), single),
            pltpu.VMEM((12, 24, depth), single),
            pltpu.VMEM((5, 10, 24, depth), single),
            pltpu.SemaphoreType.DMA((4,)),
        ],
        compiler_params=pltpu.CompilerParams(vmem_limit_bytes=vmem_small),
        name=name,
    )(*inputs)


def transport(inside, low, middle, high, to_left, to_right, above, below, before, after, flow_rows, flow_columns):
    whole = jax.ShapeDtypeStruct((species_count, rows_here, columns_here, depth), single)
    outside = pl.BlockSpec(memory_space=pl.ANY)
    done, inner = moved_call(
        inner_kernel, "inner",
        (inside, low, middle, high, to_left, to_right, before, after, flow_rows, flow_columns),
        [whole, jax.ShapeDtypeStruct((6, 18, species_count, depth), single)],
        [outside, pl.BlockSpec(memory_space=pltpu.VMEM)], [], {},
    )
    return moved_call(
        outer_kernel, "outer",
        (inside, done, inner, low, high, above, below, before, after, flow_rows, flow_columns),
        whole, outside, [pltpu.VMEM((4, 18, species_count, depth), single)], {1: 0},
    )


def onward(array, axis, by):
    length = lax.axis_size(axis)
    pairs = [(i, i + by) for i in range(length) if 0 <= i + by < length]
    return lax.ppermute(array, axis, pairs)


def on_device(species, rate_matrices, loss_rates, sweeps, flow_rows, flow_columns):
    loss = loss_rates.reshape(1, species_count)
    arguments = (species, rate_matrices, loss, sweeps)
    kept = [pltpu.with_memory_space_constraint(a, pltpu.HBM) for a in (*arguments, flow_rows, flow_columns)]
    to_left, to_right = react_edges(*kept)
    before = onward(to_right, "gy", 1)
    after = onward(to_left, "gy", -1)
    low, high = react_ends(*arguments, to_left, to_right)
    low, high = add_corners(low, high, before, after, flow_rows, flow_columns)
    above = onward(high, "gx", 1)
    below = onward(low, "gx", -1)
    middle = react_middle(*arguments)
    x, y = lax.axis_index("gx"), lax.axis_index("gy")
    inside = jnp.stack(
        [x > 0, x < lax.axis_size("gx") - 1, y > 0, y < lax.axis_size("gy") - 1]
    ).astype(jnp.int32)
    return transport(
        inside, low, middle, high, to_left, to_right, above, below, before, after, flow_rows, flow_columns
    )


def solution(mesh):
    placed = (
        P(None, "gx", "gy", None),
        P("gx", "gy", None),
        P(),
        P("gx", "gy"),
        P("gx", "gy", None),
        P("gx", "gy", None),
    )
    return jax.shard_map(
        on_device, mesh=mesh, in_specs=placed, out_specs=P(None, "gx", "gy", None), check_vma=False
    )
```
